768 devices in a mesh: dp: 16 (over y, core), section: 48 (over x, z).
Axes of the slice: x: 4, y: 8, z: 12, core: 2. Of those that a mesh axis runs over, the one named last changes fastest.
Arguments:
- lat_raw: bfloat16 [48, 16, 16, 16], P('section', None, 'dp'), may hold values from -6 to 6
- txt_raw: bfloat16 [48, 16, 16, 4096], P('section', None, 'dp'), may hold values from -6 to 6
- lat_embed: bfloat16 [16, 1024], replicated, may hold values from -1.5 to 1.5
- txt_embed: bfloat16 [4096, 1024], replicated, may hold values from -0.09375 to 0.09375
- image_owner: int32 [48, 16], replicated, may hold values from 0 to 15, each once within a row
- text_len: int32 [48, 16], replicated, may hold values from 1 to 16
- weights: bfloat16 [48, 1024, 1024], P('section', 'dp'), may hold values from -0.1875 to 0.1875
- top_grad: bfloat16 [16, 48, 32, 1024], P('dp', 'section'), may hold values from -0.75 to 0.75
Outputs:
- weight_grads: float32 [48, 1024, 1024], P('section', 'dp')
The draws below stay inside these ranges and needn't reach their ends.
Inputs may be any that keep to these rules, and one draw needn't show every extreme that they name: `image_owner`: each row names every data shard exactly once.
All inputs are finite; a program needn't handle non-finite values.
Results may differ from the reference program's by a relative error of at most 0.023.
Values may be sent and summed in bfloat16 or wider, within the bound.
A program may use at most 32 MiB of HBM per device.

```python
import jax
import jax.numpy as jnp
from jax import lax

C = 1024
TXT_IN = 4096
LAT_IN = 16
LAT = 16
TXT = 16
PIPE = 8
ROWS = 32
N_DP = 16
N_SECTION = 48


def with_ends(values, stream_key, smallest, top_value):
    place = [jax.random.randint(jax.random.fold_in(stream_key, axis), (), 0, length) for axis, length in enumerate(values.shape)]
    longest = values.shape.index(max(values.shape))
    next_to = place[:longest] + [(place[longest] + 1) % values.shape[longest]] + place[longest + 1:]
    return values.at[tuple(place)].set(smallest).at[tuple(next_to)].set(top_value)


def steps_of(rng, extent, split, low, top_value):
    factor_of, own = 1.0, jax.random.fold_in(rng, 6)
    for dim, parts in split:
        draws = jnp.exp(jax.random.uniform(jax.random.fold_in(own, dim), (parts,), jnp.float32, low / len(split), top_value / len(split)))
        factor_of = factor_of * jnp.repeat(draws, extent[dim] // parts).reshape([-1 if axis == dim else 1 for axis in range(len(extent))])
    return factor_of


def scatter_about(rng, shape, spread, bound, split=(), dtype=jnp.bfloat16):
    loudness = steps_of(rng, shape, split, -0.22, 0.18) if split else 1.0
    array = jax.random.normal(rng, shape, jnp.float32) * spread * loudness
    return jnp.minimum(jnp.maximum(array, -bound), bound).astype(dtype)


def setup_inputs(seed: int = 0) -> dict:
    key_of = jax.random.split(jax.random.key(seed), 9)
    lat_raw = scatter_about(key_of[0], (N_SECTION, N_DP, LAT, LAT_IN), 1.0, 6.0, ((0, 48), (2, 16)))
    txt_raw = scatter_about(key_of[1], (N_SECTION, N_DP, TXT, TXT_IN), 1.0, 6.0, ((0, 48), (2, 16)))
    lat_embed = scatter_about(key_of[2], (LAT_IN, C), LAT_IN ** -0.5, 1.5)
    txt_embed = scatter_about(key_of[3], (TXT_IN, C), TXT_IN ** -0.5, 0.09375)
    image_owner = jax.vmap(lambda own: jax.random.permutation(own, N_DP))(jax.random.split(key_of[4], N_SECTION)).reshape((N_SECTION, N_DP)).astype(jnp.int32)
    text_len = with_ends(jax.random.randint(key_of[5], (N_SECTION, N_DP), 1, TXT + 1), jax.random.fold_in(key_of[5], 1), 1, TXT).astype(jnp.int32)
    weights = scatter_about(key_of[6], (N_SECTION, C, C), C ** -0.5, 0.1875, ((0, 48), (1, 16)))
    top_grad = scatter_about(key_of[7], (N_DP, N_SECTION, ROWS, C), 0.05, 0.75, ((0, 16), (1, 48)))
    return dict(lat_raw=lat_raw, txt_raw=txt_raw, lat_embed=lat_embed, txt_embed=txt_embed, image_owner=image_owner, text_len=text_len, weights=weights, top_grad=top_grad)


norm_eps = 1e-06

def modulate(tokens_in, text_mask, text_count):
    inv_norm = lax.rsqrt(lax.optimization_barrier(jnp.mean(tokens_in * tokens_in, axis=1, keepdims=True)) + norm_eps)
    normed = tokens_in * inv_norm
    pooled = 0.5 * lax.optimization_barrier(jnp.sum(normed * text_mask[:, None], axis=0)) / text_count
    return normed * (1.0 + pooled)[None, :]

def silu_slope(gate_preactivation):
    sigmoid_v = jax.nn.sigmoid(gate_preactivation)
    return sigmoid_v * (1.0 + gate_preactivation * (1.0 - sigmoid_v))

def reference(lat_raw, txt_raw, lat_embed, txt_embed, image_owner, text_len, weights, top_grad):
    lat_enc = jnp.einsum('sjrc,cf->sjrf', lat_raw.astype(jnp.float32), lat_embed.astype(jnp.float32)).astype(jnp.bfloat16)
    text_enc = jnp.einsum('sjrc,cf->sjrf', txt_raw.astype(jnp.float32), txt_embed.astype(jnp.float32)).astype(jnp.bfloat16)
    images = jnp.concatenate([lat_enc, text_enc], axis=2)
    senders = jnp.argsort(image_owner, axis=1, stable=True).astype(jnp.int32)
    positions = jnp.arange(LAT + TXT).astype(jnp.int32)
    batch_mod = jax.vmap(modulate)
    micro_range = jnp.arange(PIPE).astype(jnp.int32)
    results = []
    for group_idx in range(N_SECTION // PIPE):
        first_col = group_idx * PIPE
        lane_images = images[first_col:first_col + PIPE]
        lane_send = senders[first_col:first_col + PIPE]
        lane_len = text_len[first_col:first_col + PIPE].astype(jnp.int32)
        portion_weight = weights[first_col:first_col + PIPE].astype(jnp.float32)
        lane_tops = top_grad[:, first_col:first_col + PIPE]

        def one_lane(total_grad, my_shard):
            src_slots = lane_send[:, my_shard]
            current = lane_images[micro_range, src_slots]
            lengths = lane_len[micro_range, src_slots]
            text_masks = ((positions[None, :] >= LAT) & (positions[None, :] < LAT + lengths[:, None])).astype(jnp.float32)
            counts = lengths.astype(jnp.float32)
            top_rows = lax.dynamic_index_in_dim(lane_tops, my_shard, 0, keepdims=False)[::-1]
            inputs = []
            for portion_index in range(PIPE):
                inputs.append(current)
                widened = current.astype(jnp.float32)
                hidden_layer_state = batch_mod(widened, text_masks, counts).astype(jnp.bfloat16)
                gate_preactivation = jnp.einsum('xat,tg->xag', hidden_layer_state.astype(jnp.float32), portion_weight[portion_index])
                current = (widened + jax.nn.silu(gate_preactivation)).astype(jnp.bfloat16)
            grad_rows = top_rows
            portion_gradient = []
            for portion_index in reversed(range(PIPE)):
                widened = inputs[portion_index].astype(jnp.float32)
                hidden_wide, pullback = jax.vjp(lambda values: batch_mod(values, text_masks, counts), widened)
                hidden_layer_state = hidden_wide.astype(jnp.bfloat16)
                gate_preactivation = jnp.einsum('xat,tg->xag', hidden_layer_state.astype(jnp.float32), portion_weight[portion_index])
                derivative_rows = (grad_rows.astype(jnp.float32) * silu_slope(gate_preactivation)).astype(jnp.bfloat16)
                portion_gradient.append(jnp.einsum('xza,xzi->ai', hidden_layer_state.astype(jnp.float32), derivative_rows.astype(jnp.float32)))
                reverse_sweep = jnp.einsum('adp,lp->adl', derivative_rows.astype(jnp.float32), portion_weight[portion_index])
                grad_rows = (grad_rows.astype(jnp.float32) + pullback(reverse_sweep)[0]).astype(jnp.bfloat16)
            return (total_grad + jnp.stack(portion_gradient[::-1]), None)
        total_grad, _ = lax.scan(one_lane, jnp.zeros((PIPE, C, C), jnp.float32), jnp.arange(N_DP).astype(jnp.int32))
        results.append(total_grad)
    return jnp.concatenate(results, axis=0)
```

```python
import functools

import jax
import jax.numpy as jnp
from jax import lax
from jax.experimental import pallas as pl
from jax.experimental.pallas import tpu as pltpu
from jax.sharding import PartitionSpec as P

PIPE = 8
EPS = 1e-06
MESH = pl.DeviceIdType.MESH
F32 = jnp.float32
BF16 = jnp.bfloat16
CHUNKS = 8
HALVES = 2


def dot(a, b, ca=1, cb=0):
    return lax.dot_general(a, b, (((ca,), (cb,)), ((), ())), preferred_element_type=F32)


def kernel(
    n_dp,
    lat_ref,
    txt_ref,
    late_ref,
    txte_ref,
    own_ref,
    len_ref,
    w_ref,
    top_ref,
    out_ref,
    txte,
    wfull,
    stage_src,
    stage_dst,
    image,
    maskw,
    x_in,
    x_out,
    g_in,
    g_out,
    hid,
    slp,
    slope_s,
    u_s,
    r_s,
    q_s,
    dw,
    pair_src,
    pair_dst,
    ring_src,
    ring_dst,
    txte_sem,
    own_sem,
    agr_send,
    agr_recv,
    agl_send,
    agl_recv,
    agp_send,
    agp_recv,
    a2a_send,
    a2a_recv,
    x_send,
    x_recv,
    g_send,
    g_recv,
    feed_send,
    top_send,
    pr_send,
    pr_recv,
    rr_send,
    rr_recv,
    rl_send,
    rl_recv,
):
    ny = n_dp // 2
    n_right = ny // 2
    n_left = ny - 1 - n_right
    dp = lax.axis_index("dp")
    sec = lax.axis_index("section")
    pos = lax.rem(sec, PIPE)
    first = sec - pos
    y = lax.div(dp, 2)
    c = lax.rem(dp, 2)
    partner = 2 * y + (1 - c)
    up = 2 * lax.rem(y + 1, ny) + c
    down = 2 * lax.rem(y + ny - 1, ny) + c
    rows = w_ref.shape[0]
    width = w_ref.shape[1]
    sub = rows // HALVES
    chunk = txte_ref.shape[0] // CHUNKS

    barrier = pltpu.get_barrier_semaphore()

    def greet_dp(k, carry):
        pl.semaphore_signal(
            barrier,
            inc=1,
            device_id={"dp": lax.rem(dp + k, n_dp), "section": sec},
            device_id_type=MESH,
        )
        return carry

    def greet_sec(k, carry):
        pl.semaphore_signal(
            barrier,
            inc=1,
            device_id={"dp": dp, "section": first + lax.rem(pos + k, PIPE)},
            device_id_type=MESH,
        )
        return carry

    lax.fori_loop(1, n_dp, greet_dp, 0)
    lax.fori_loop(1, PIPE, greet_sec, 0)

    def embed_copy(i):
        return pltpu.make_async_copy(
            txte_ref.at[pl.ds(i * chunk, chunk)], txte.at[pl.ds(i * chunk, chunk)], txte_sem.at[i]
        )

    for i in range(CHUNKS):
        embed_copy(i).start()

    def at_dp(d):
        return {"dp": d, "section": sec}

    def at_pos(k):
        return {"dp": dp, "section": first + k}

    def w_rows(block, h):
        return wfull.at[pl.ds(pl.multiple_of(block * rows + h * sub, sub), sub)]

    own_copy = pltpu.make_async_copy(
        w_ref, wfull.at[pl.ds(pl.multiple_of(dp * rows, rows), rows)], own_sem
    )
    own_copy.start()

    owners = own_ref[...]
    lane = lax.broadcasted_iota(jnp.int32, owners.shape, 1)
    owner_col = jnp.sum(jnp.where(lane == sec, owners, 0), axis=1, keepdims=True)
    pick = (
        owner_col == lax.broadcasted_iota(jnp.int32, (n_dp, n_dp), 1)
    ).astype(F32)
    counts = jnp.sum(jnp.where(owners == dp, len_ref[...], 0), axis=0, keepdims=True)
    lane_row = lax.broadcasted_iota(jnp.int32, counts.shape, 1)
    half_rows = image.shape[0] // 2
    place = lax.broadcasted_iota(jnp.int32, (image.shape[0], 128), 0) - half_rows

    def mask_step(m, carry):
        count = jnp.sum(jnp.where(lane_row == first + m, counts, 0), axis=1, keepdims=True)
        inside = (place >= 0) & (place < count)
        maskw[m] = jnp.where(inside, 0.5 / count.astype(F32), 0.0)
        return carry

    lax.fori_loop(0, PIPE, mask_step, 0)

    lat_enc = dot(lat_ref[...], late_ref[...]).astype(BF16)

    acc = jnp.zeros((n_dp, width), F32)
    for i in range(CHUNKS):
        embed_copy(i).wait()
        acc += dot(txt_ref[:, i * chunk : (i + 1) * chunk], txte[i * chunk : (i + 1) * chunk, :])
    pick = pick.astype(BF16)
    stage_src[:, 0, 0:width] = dot(pick, lat_enc, 0, 0)
    stage_src[:, 0, width : 2 * width] = dot(pick, acc.astype(BF16), 0, 0)

    pl.semaphore_wait(barrier, n_dp - 1 + PIPE - 1)

    def right_copy(t, h):
        block = 2 * lax.rem(y + ny - t, ny) + c
        src = w_ref.at[pl.ds(h * sub, sub)] if t == 0 else w_rows(block, h)
        return pltpu.make_async_remote_copy(
            src, w_rows(block, h), agr_send.at[t, h], agr_recv.at[t, h], at_dp(up), MESH
        )

    def left_copy(t, h):
        block = 2 * lax.rem(y + t, ny) + c
        src = w_ref.at[pl.ds(h * sub, sub)] if t == 0 else w_rows(block, h)
        return pltpu.make_async_remote_copy(
            src, w_rows(block, h), agl_send.at[t, h], agl_recv.at[t, h], at_dp(down), MESH
        )

    def pair_copy(i, block_y, h):
        block = 2 * block_y + c
        src = w_ref.at[pl.ds(h * sub, sub)] if i == 0 else w_rows(block, h)
        return pltpu.make_async_remote_copy(
            src, w_rows(block, h), agp_send.at[i, h], agp_recv.at[i, h], at_dp(partner), MESH
        )

    def from_right_going(t):
        return lax.rem(y + ny - t, ny)

    def from_left_going(t):
        return lax.rem(y + t, ny)

    def gather_step(t):
        for h in range(HALVES):
            if t > 0:
                right_copy(t - 1, h).wait_recv()
            if t < n_right:
                right_copy(t, h).start()
            if t > 0:
                pair_copy(t, from_right_going(t), h).start()
            if t == 0:
                pair_copy(0, y, h).start()
            if 0 < t <= n_left:
                left_copy(t - 1, h).wait_recv()
            if t < n_left:
                left_copy(t, h).start()
            if 0 < t <= n_left:
                pair_copy(n_right + t, from_left_going(t), h).start()

    gather_step(0)

    def exchange(k):
        dest = lax.rem(dp + k, n_dp)
        return pltpu.make_async_remote_copy(
            stage_src.at[dest],
            stage_dst.at[dp],
            a2a_send.at[k],
            a2a_recv.at[k],
            at_dp(dest),
            MESH,
        )

    keep = pltpu.make_async_copy(stage_src.at[dp], stage_dst.at[dp], a2a_recv.at[0])
    keep.start()

    def exchange_start(k, carry):
        exchange(k).start()
        return carry

    lax.fori_loop(1, n_dp, exchange_start, 0)

    def top_copy():
        return pltpu.make_async_remote_copy(
            top_ref,
            g_in.at[PIPE - 1 - pos],
            top_send,
            g_recv.at[PIPE - 1 - pos],
            at_pos(PIPE - 1),
            MESH,
        )

    @pl.when(pos == PIPE - 1)
    def _():
        pltpu.make_async_copy(top_ref, g_in.at[0], g_recv.at[0]).start()

    @pl.when(pos != PIPE - 1)
    def _():
        top_copy().start()

    def exchange_wait(k, carry):
        exchange(k).wait_recv()
        return carry

    lax.fori_loop(1, n_dp, exchange_wait, 0)
    keep.wait()
    image[0:half_rows, :] = stage_dst[:, 0, 0:width].astype(BF16)
    image[half_rows : 2 * half_rows, :] = stage_dst[:, 0, width : 2 * width].astype(BF16)

    def feed_copy():
        return pltpu.make_async_remote_copy(
            image, x_in.at[pos], feed_send, x_recv.at[pos], at_pos(0), MESH
        )

    @pl.when(pos == 0)
    def _():
        pltpu.make_async_copy(image, x_in.at[0], x_recv.at[0]).start()

    @pl.when(pos != 0)
    def _():
        feed_copy().start()

    for t in range(1, n_right + 1):
        gather_step(t)
    own_copy.wait()
    for i in range(ny):
        for h in range(HALVES):
            pair_copy(i, y, h).wait_recv()

    span = width // HALVES

    def x_copy(m, h):
        cols = pl.ds(h * span, span)
        return pltpu.make_async_remote_copy(
            x_out.at[m, :, cols],
            x_in.at[m, :, cols],
            x_send.at[m],
            x_recv.at[m],
            at_pos(lax.rem(pos + 1, PIPE)),
            MESH,
        )

    def x_whole(m):
        return pltpu.make_async_remote_copy(
            x_out.at[m], x_in.at[m], x_send.at[m], x_recv.at[m], at_pos(lax.rem(pos + 1, PIPE)), MESH
        )

    def g_copy(m):
        return pltpu.make_async_remote_copy(
            g_out.at[m],
            g_in.at[m],
            g_send.at[m],
            g_recv.at[m],
            at_pos(lax.rem(pos + PIPE - 1, PIPE)),
            MESH,
        )

    depth = image.shape[0]

    def band(m):
        return pl.ds(pl.multiple_of(m * depth, depth), depth)

    def forward(m):
        x_whole(m).wait_recv()
        x = x_in[m].astype(F32)
        r = lax.rsqrt(jnp.mean(x * x, axis=1, keepdims=True) + EPS)
        u = x * r
        mask = maskw[m][:, 0:1]
        q = 1.0 + jnp.sum(u * mask, axis=0, keepdims=True)
        h = (u * q).astype(BF16)
        u_s[m] = u
        r_s[m] = jnp.broadcast_to(r, (depth, 128))
        q_s[m] = q
        hid[band(m), :] = h
        for half in range(HALVES):
            cols = slice(half * span, (half + 1) * span)
            pre = dot(h, wfull[:, cols])
            gate = 0.5 * jnp.tanh(0.5 * pre) + 0.5
            slope_s[m, :, cols] = gate * (1.0 + pre * (1.0 - gate))

            @pl.when(pos < PIPE - 1)
            def _():
                x_out[m, :, cols] = (x[:, cols] + pre * gate).astype(BF16)
                x_copy(m, half).start()

    def backward(m):
        g_copy(m).wait_recv()
        g = g_in[m].astype(F32)
        slope = (g * slope_s[m]).astype(BF16)
        slp[band(m), :] = slope

        @pl.when(pos > 0)
        def _():
            b = dot(slope, wfull[...], 1, 1)
            u = u_s[m]
            mask = maskw[m][:, 0:1]
            r = r_s[m][:, 0:1]
            du = b * q_s[m] + mask * jnp.sum(b * u, axis=0, keepdims=True)
            mean = jnp.mean(du * u, axis=1, keepdims=True)
            g_out[m] = (g + r * (du - u * mean)).astype(BF16)
            g_copy(m).start()

    lag = jnp.where(pos == PIPE - 1, 0, jnp.where(pos == PIPE - 2, 5, PIPE))

    def turn(t, carry):
        @pl.when(t < PIPE)
        def _():
            forward(t)

        @pl.when((t >= lag) & (t < lag + PIPE))
        def _():
            backward(t - lag)

        return carry

    lax.fori_loop(0, 2 * PIPE, turn, 0)

    def target(i):
        if i == ny - 1:
            return y
        if i % 2 == 0:
            return lax.rem(y + n_right - i // 2, ny)
        return lax.rem(y + ny - n_left + i // 2, ny)

    def pr_copy(i):
        return pltpu.make_async_remote_copy(
            pair_src.at[i], pair_dst.at[i], pr_send.at[i], pr_recv.at[i], at_dp(partner), MESH
        )

    def mine(i, h):
        base = pl.multiple_of(target(i) * 2 * rows + c * rows + h * sub, sub)
        return dw[pl.ds(base, sub), :] + pair_dst[i, h * sub : (h + 1) * sub, :].astype(F32)

    for i in range(ny):
        block = target(i)
        at = pl.multiple_of(block * 2 * rows, 2 * rows)
        dw[pl.ds(at, 2 * rows), :] = dot(hid[:, pl.ds(at, 2 * rows)], slp[...], 0, 0)
        theirs = pl.multiple_of(block * 2 * rows + (1 - c) * rows, rows)
        pair_src[i] = dw[pl.ds(theirs, rows), :].astype(BF16)
        pr_copy(i).start()

    def rr_copy(t, h):
        part = pl.ds(h * sub, sub)
        return pltpu.make_async_remote_copy(
            ring_src.at[2 * t, part],
            ring_dst.at[2 * t, part],
            rr_send.at[t, h],
            rr_recv.at[t, h],
            at_dp(up),
            MESH,
        )

    def rl_copy(t, h):
        part = pl.ds(h * sub, sub)
        return pltpu.make_async_remote_copy(
            ring_src.at[2 * t + 1, part],
            ring_dst.at[2 * t + 1, part],
            rl_send.at[t, h],
            rl_recv.at[t, h],
            at_dp(down),
            MESH,
        )

    def arrived(slot, h):
        return ring_dst[slot, h * sub : (h + 1) * sub, :].astype(F32)

    for t in range(n_right):
        pr_copy(2 * t).wait_recv()
        if t < n_left:
            pr_copy(2 * t + 1).wait_recv()
        for h in range(HALVES):
            total = mine(2 * t, h)
            if t > 0:
                rr_copy(t - 1, h).wait_recv()
                total = total + arrived(2 * (t - 1), h)
            ring_src[2 * t, h * sub : (h + 1) * sub, :] = total.astype(BF16)
            rr_copy(t, h).start()
            if t < n_left:
                total = mine(2 * t + 1, h)
                if t > 0:
                    rl_copy(t - 1, h).wait_recv()
                    total = total + arrived(2 * (t - 1) + 1, h)
                ring_src[2 * t + 1, h * sub : (h + 1) * sub, :] = total.astype(BF16)
                rl_copy(t, h).start()
    pr_copy(ny - 1).wait_recv()
    for h in range(HALVES):
        total = mine(ny - 1, h)
        rl_copy(n_left - 1, h).wait_recv()
        total = total + arrived(2 * (n_left - 1) + 1, h)
        rr_copy(n_right - 1, h).wait_recv()
        total = total + arrived(2 * (n_right - 1), h)
        out_ref[h * sub : (h + 1) * sub, :] = total

    for h in range(HALVES):
        for t in range(n_right):
            right_copy(t, h).wait_send()
            rr_copy(t, h).wait_send()
        for t in range(n_left):
            left_copy(t, h).wait_send()
            rl_copy(t, h).wait_send()
        for i in range(ny):
            pair_copy(i, y, h).wait_send()
    for i in range(ny):
        pr_copy(i).wait_send()

    def exchange_sent(k, carry):
        exchange(k).wait_send()
        return carry

    lax.fori_loop(1, n_dp, exchange_sent, 0)

    @pl.when(pos != PIPE - 1)
    def _():
        top_copy().wait_send()

        def sent(m, carry):
            x_whole(m).wait_send()
            return carry

        lax.fori_loop(0, PIPE, sent, 0)

    @pl.when(pos != 0)
    def _():
        feed_copy().wait_send()

        def sent(m, carry):
            g_copy(m).wait_send()
            return carry

        lax.fori_loop(0, PIPE, sent, 0)


def local(n_dp, lat_raw, txt_raw, lat_embed, txt_embed, image_owner, text_len, weights, top_grad):
    lat = lat_raw.reshape(lat_raw.shape[1], lat_raw.shape[3])
    txt = txt_raw.reshape(txt_raw.shape[1], txt_raw.shape[3])
    w = weights[0]
    top = top_grad[0, 0]
    rows, width = w.shape
    depth = top.shape[0]
    ny = n_dp // 2
    n_right = ny // 2
    n_left = ny - 1 - n_right
    vmem = pl.BlockSpec(memory_space=pltpu.VMEM)
    dma = pltpu.SemaphoreType.DMA
    out = pl.pallas_call(
        functools.partial(kernel, n_dp),
        out_shape=jax.ShapeDtypeStruct((rows, width), F32),
        in_specs=[
            vmem,
            vmem,
            vmem,
            pl.BlockSpec(memory_space=pl.ANY),
            vmem,
            vmem,
            vmem,
            vmem,
        ],
        out_specs=vmem,
        scratch_shapes=[
            pltpu.VMEM(txt_embed.shape, BF16),
            pltpu.VMEM((width, width), BF16),
            pltpu.VMEM((n_dp, 1, 2 * width), F32),
            pltpu.VMEM((n_dp, 1, 2 * width), F32),
            pltpu.VMEM((depth, width), BF16),
            pltpu.VMEM((PIPE, depth, 128), F32),
            pltpu.VMEM((PIPE, depth, width), BF16),
            pltpu.VMEM((PIPE, depth, width), BF16),
            pltpu.VMEM((PIPE, depth, width), BF16),
            pltpu.VMEM((PIPE, depth, width), BF16),
            pltpu.VMEM((PIPE * depth, width), BF16),
            pltpu.VMEM((PIPE * depth, width), BF16),
            pltpu.VMEM((PIPE, depth, width), F32),
            pltpu.VMEM((PIPE, depth, width), F32),
            pltpu.VMEM((PIPE, depth, 128), F32),
            pltpu.VMEM((PIPE, 1, width), F32),
            pltpu.VMEM((width, width), F32),
            pltpu.VMEM((ny, rows, width), BF16),
            pltpu.VMEM((ny, rows, width), BF16),
            pltpu.VMEM((ny - 1, rows, width), BF16),
            pltpu.VMEM((ny - 1, rows, width), BF16),
            dma((CHUNKS,)),
            dma,
            dma((n_right, HALVES)),
            dma((n_right, HALVES)),
            dma((n_left, HALVES)),
            dma((n_left, HALVES)),
            dma((ny, HALVES)),
            dma((ny, HALVES)),
            dma((n_dp,)),
            dma((n_dp,)),
            dma((PIPE,)),
            dma((PIPE,)),
            dma((PIPE,)),
            dma((PIPE,)),
            dma,
            dma,
            dma((ny,)),
            dma((ny,)),
            dma((n_right, HALVES)),
            dma((n_right, HALVES)),
            dma((n_left, HALVES)),
            dma((n_left, HALVES)),
        ],
        compiler_params=pltpu.CompilerParams(
            collective_id=0, has_side_effects=True, vmem_limit_bytes=56 * 1024 * 1024
        ),
        name="cascade",
    )(lat, txt, lat_embed, txt_embed, image_owner.T, text_len.T, w, top)
    return out[None]


def solution(mesh):
    placed = (
        P("section", None, "dp", None),
        P("section", None, "dp", None),
        P(),
        P(),
        P(),
        P(),
        P("section", "dp", None),
        P("dp", "section", None, None),
    )
    return jax.shard_map(
        functools.partial(local, mesh.shape["dp"]),
        mesh=mesh,
        in_specs=placed,
        out_specs=P("section", "dp", None),
        check_vma=False,
    )
```
